256 devices in a mesh: fsdp: 16 (over y_lo, z), dp: 16 (over x, y_hi, core).
Axes of the slice: x: 4, y: 4 (y_hi: 2, y_lo: 2; y = y_hi * 2 + y_lo), z: 8, core: 2. Of those that a mesh axis runs over, the one named last changes fastest.
Arguments:
- patch_acts: bfloat16 [32768, 12288], P(('fsdp', 'dp')), may hold values from -6 to 6
- patch_slot: int32 [32768], P(('fsdp', 'dp')), may hold values from 0 to 1024, as said below
- out_grads: bfloat16 [16384, 3072], P(('fsdp', 'dp')), may hold values from -6 to 6
- latent_weight: bfloat16 [12288, 3072], P('dp', 'fsdp'), may hold values from -0.0546875 to 0.0546875
- step_size: bfloat16 [1, 3072], P(None, 'fsdp')
Outputs:
- grad_acts: bfloat16 [32768, 12288], P(('fsdp', 'dp'))
- grad_weight: float32 [12288, 3072], P('dp', 'fsdp')
- grad_step: float32 [1, 3072], P(None, 'fsdp')
The draws below stay inside these ranges and needn't reach their ends.
Inputs may be any that keep to these rules, and one draw needn't show every extreme that they name: `patch_slot`: within each fsdp index, the used patch rows of every image owner come first in its 128 slots and carry a packed row below 1024, the others carry 1024; each packed row of the fsdp index receives exactly one patch row; in every fsdp index some image owner has all 128 slots used.
All inputs are finite; a program needn't handle non-finite values.
Results may differ from the reference program's by a relative error of at most 0.0049.
Values may be sent and summed in bfloat16 or wider, within the bound.
No kernel may reach another device: no remote copies, remote signals or barrier semaphores. Data moves between devices by JAX's collectives and lax.ppermute only.
A program may use at most 128 MiB of HBM per device.

```python
import jax
import jax.numpy as jnp

D_W = 3072
FF_W = 12288
PATCH_CAP = 128
ROWS = 1024
ALL_PATCH = 32768
ALL_ROWS = 16384
N_FSDP = 16
N_DP = 16


def draw_step_size(key, part):
    base_step = FF_W ** (-0.5)
    spread = jax.random.uniform(key, (1, D_W), jnp.float32)
    return (base_step * jnp.exp(jnp.log(0.25) + spread * jnp.log(10.0))).astype(jnp.bfloat16)


def draw_patch_slot(key, part):
    half_cap = PATCH_CAP // 2
    group_rows = half_cap * N_DP

    def one_group(group_key):
        first_key, second_key, third_key = jax.random.split(group_key, 3)
        order = jax.random.permutation(first_key, N_DP).astype(jnp.int32)
        extra = jax.random.randint(second_key, (N_DP // 2,), 0, half_cap + 1).astype(jnp.int32)
        extra = extra.at[0].set(half_cap)
        shifted = jnp.zeros((N_DP,), jnp.int32).at[order[0::2]].set(extra).at[order[1::2]].set(-extra)
        counts = half_cap + shifted
        positions = jnp.arange(PATCH_CAP, dtype=jnp.int32)
        valid = (positions[None, :] < counts[:, None]).astype(jnp.int32).reshape(-1)
        ranking = jnp.cumsum(valid) - 1
        shuffled = jax.random.permutation(third_key, group_rows).astype(jnp.int32)
        chosen = shuffled[jnp.clip(ranking, 0, group_rows - 1)]
        return jnp.where(valid == 1, chosen, group_rows).astype(jnp.int32)
    group_keys = jax.random.split(key, N_FSDP)
    return jax.vmap(one_group)(group_keys).reshape(-1).astype(jnp.int32)


def levels(key, shape, shards, low, largest):
    def one(dim, blocks):
        heights = jax.random.uniform(jax.random.fold_in(jax.random.fold_in(key, 6), dim), (blocks,), jnp.float32, low / len(shards), largest / len(shards))
        return jnp.repeat(jnp.exp(heights), shape[dim] // blocks).reshape((-1,) + (1,) * (len(shape) - dim - 1))

    factor_of = one(*shards[0])
    for cut in shards[1:]:
        factor_of = factor_of * one(*cut)
    return factor_of


def scatter_about(stream_key, dims, scale, limit, cuts=(), held_as=jnp.bfloat16):
    array = scale * jax.random.normal(stream_key, dims, jnp.float32)
    if cuts:
        array = array * levels(stream_key, dims, cuts, -0.22, 0.18)
    return jnp.clip(array, -limit, limit).astype(held_as)


def setup_inputs(seed: int = 0) -> dict:
    key_of = jax.random.split(jax.random.key(seed), 6)
    return {
        "patch_acts": scatter_about(key_of[0], (ALL_PATCH, FF_W), 1.0, 6.0, ((0, 256),)),
        "patch_slot": draw_patch_slot(jax.random.fold_in(key_of[5], 71), 0),
        "out_grads": scatter_about(key_of[2], (ALL_ROWS, D_W), 1.0, 6.0, ((0, 256),)),
        "latent_weight": scatter_about(key_of[3], (FF_W, D_W), FF_W ** -0.5, 0.0546875, ((0, 16), (1, 16))),
        "step_size": draw_step_size(jax.random.fold_in(key_of[5], 71), 0),
    }


top_level = 7.0
wobble = 0.9
two_pi = 6.283185307179586
inv_root_two = 0.7071067811865476
inv_root_tau = 0.3989422804014327


def gelu_pair(values):
    normal_cdf = 0.5 * (1.0 + jax.scipy.special.erf(values * inv_root_two))
    density = jnp.exp(-0.5 * values * values) * inv_root_tau
    return values * normal_cdf, normal_cdf + values * density


def soft_quantize(weight, step):
    ratio = weight / step
    clipped = top_level * jnp.tanh(ratio / top_level)
    phase = two_pi * clipped
    quantized = clipped - wobble * jnp.sin(phase) / two_pi
    slope = (1.0 - wobble * jnp.cos(phase)) * (1.0 - (clipped / top_level) * (clipped / top_level))
    return quantized, slope, ratio


def reference(patch_acts, patch_slot, out_grads, latent_weight, step_size):
    group_slots = patch_slot.reshape(N_FSDP, N_DP * PATCH_CAP).astype(jnp.int32)
    offsets = (jnp.arange(N_FSDP, dtype=jnp.int32) * (ROWS + 1))[:, None]
    target = (offsets + group_slots).reshape(-1).astype(jnp.int32)
    holder = jnp.zeros((N_FSDP * (ROWS + 1), FF_W), jnp.bfloat16).at[target].set(patch_acts)
    packed = holder.reshape(N_FSDP, ROWS + 1, FF_W)[:, :ROWS].reshape(N_FSDP * ROWS, FF_W)
    act_full, gelu_slope = gelu_pair(packed.astype(jnp.float32))
    act = act_full.astype(jnp.bfloat16)
    step_full = step_size.astype(jnp.float32)
    quantized, slope, ratio = soft_quantize(latent_weight.astype(jnp.float32), step_full)
    qweight = (step_full * quantized).astype(jnp.bfloat16)
    grad_hidden = jnp.dot(out_grads, qweight.T, preferred_element_type=jnp.float32)
    grad_packed = (grad_hidden * gelu_slope).astype(jnp.bfloat16)
    padded = jnp.concatenate([grad_packed.reshape(N_FSDP, ROWS, FF_W), jnp.zeros((N_FSDP, 1, FF_W), jnp.bfloat16)], axis=1)
    grad_acts = padded.reshape(N_FSDP * (ROWS + 1), FF_W)[target]
    grad_qweight = jnp.dot(act.T, out_grads, preferred_element_type=jnp.float32)
    grad_weight = grad_qweight * slope
    scale_factor = (FF_W * top_level) ** -0.5
    grad_step = scale_factor * jnp.sum(grad_qweight * (quantized - ratio * slope), axis=0, keepdims=True)
    return grad_acts, grad_weight, grad_step
```

```python
import functools

import jax
import jax.numpy as jnp
from jax import lax
from jax.experimental import pallas as pl
from jax.experimental.pallas import tpu as pltpu
from jax.sharding import Mesh, PartitionSpec as P

FF_W = 12288

top_level = 7.0
wobble = 0.9
two_pi = 6.283185307179586
inv_root_two = 0.7071067811865476
inv_root_tau = 0.3989422804014327

PARTS = ("a", "z", "x", "b", "c")
SIZES = (2, 8, 4, 2, 2)
FSDP = ("a", "z")
DP = ("x", "b", "c")
SWAP = [(0, 1), (1, 0)]

VMEM_LIMIT = 56 * 1024 * 1024


def gelu_pair(values):
    normal_cdf = 0.5 * (1.0 + lax.erf(values * inv_root_two))
    density = jnp.exp(-0.5 * values * values) * inv_root_tau
    return (values * normal_cdf, normal_cdf + values * density)


def soft_quantize(weight, step):
    ratio = weight / step
    clipped = top_level * jnp.tanh(ratio / top_level)
    phase = two_pi * clipped
    quantized = clipped - wobble * jnp.sin(phase) / two_pi
    slope = (1.0 - wobble * jnp.cos(phase)) * (1.0 - clipped / top_level * (clipped / top_level))
    return (quantized, slope, ratio)


def swap(value, axis):
    return lax.ppermute(value, axis, SWAP)


def shift(value, axis, by):
    count = lax.axis_size(axis)
    return lax.ppermute(value, axis, [(i, (i + by) % count) for i in range(count)])


def copy_block(source, target):
    target[...] = source[...].reshape(target.shape)


def split_columns(values, count):
    rows, width = values.shape[0], values.shape[1] // count
    return pl.pallas_call(
        copy_block,
        grid=(count,),
        in_specs=[pl.BlockSpec((rows, width), lambda i: (0, i))],
        out_specs=pl.BlockSpec((1, rows, width), lambda i: (i, 0, 0)),
        out_shape=jax.ShapeDtypeStruct((count, rows, width), values.dtype),
        name="split_columns",
    )(values)


def join_columns(values):
    count, rows, width = values.shape
    return pl.pallas_call(
        copy_block,
        grid=(count,),
        in_specs=[pl.BlockSpec((1, rows, width), lambda i: (i, 0, 0))],
        out_specs=pl.BlockSpec((rows, width), lambda i: (0, i)),
        out_shape=jax.ShapeDtypeStruct((rows, count * width), values.dtype),
        name="join_columns",
    )(values)


def weight_grad_body(place, incoming, grads, packed, out, act):
    rows = packed.shape[0]

    @pl.when(pl.program_id(0) == 0)
    def _():
        slots = incoming.shape[0]
        part = rows // 4
        for k in range(4):
            here = pl.ds(k * part, part)
            row = k * part + lax.broadcasted_iota(jnp.int32, (part, slots), 0)
            pick = (row == place[...]).astype(jnp.bfloat16)
            found = jnp.dot(pick, incoming[...], preferred_element_type=jnp.float32)
            packed[here, :] = found.astype(jnp.bfloat16)
            act[here, :] = gelu_pair(found)[0].astype(jnp.bfloat16)

    out[...] = lax.dot_general(
        grads[...], act[...], (((0,), (0,)), ((), ())), preferred_element_type=jnp.float32
    )


def weight_grad(place, incoming, grads):
    rows, outputs = grads.shape
    slots, hidden = incoming.shape
    tile = 384
    return pl.pallas_call(
        weight_grad_body,
        grid=(outputs // tile,),
        in_specs=[
            pl.BlockSpec((1, slots), lambda i: (0, 0)),
            pl.BlockSpec((slots, hidden), lambda i: (0, 0), pipeline_mode=pl.Buffered(1)),
            pl.BlockSpec((rows, tile), lambda i: (0, i)),
        ],
        out_specs=[
            pl.BlockSpec((rows, hidden), lambda i: (0, 0)),
            pl.BlockSpec((tile, hidden), lambda i: (i, 0)),
        ],
        out_shape=[
            jax.ShapeDtypeStruct((rows, hidden), jnp.bfloat16),
            jax.ShapeDtypeStruct((outputs, hidden), jnp.float32),
        ],
        scratch_shapes=[pltpu.VMEM((rows, hidden), jnp.bfloat16)],
        compiler_params=pltpu.CompilerParams(vmem_limit_bytes=VMEM_LIMIT),
        cost_estimate=pl.CostEstimate(
            flops=2 * rows * hidden * (outputs + slots),
            bytes_accessed=2 * rows * outputs + 4 * outputs * hidden + 2 * slots * hidden,
            transcendentals=rows * hidden,
        ),
        name="weight_grad",
    )(place, incoming, grads)


def hidden_grad_body(place, grads, weight, packed, out, pick):
    rows = packed.shape[0]
    slots = place.shape[0]

    @pl.when(pl.program_id(0) == 0)
    def _():
        column = lax.broadcasted_iota(jnp.int32, (slots, rows), 1)
        pick[...] = (column == place[...]).astype(jnp.bfloat16)

    grad = jnp.dot(grads[...], weight[...], preferred_element_type=jnp.float32)
    slope = gelu_pair(packed[...].astype(jnp.float32))[1]
    grad = (grad * slope).astype(jnp.bfloat16)
    found = jnp.dot(pick[...], grad, preferred_element_type=jnp.float32)
    out[...] = found.astype(jnp.bfloat16).reshape(out.shape)


def hidden_grad(place, grads, weight, packed, owners):
    rows, outputs = grads.shape
    hidden = packed.shape[1]
    slots = place.shape[0]
    tile = 256
    return pl.pallas_call(
        hidden_grad_body,
        grid=(hidden // tile,),
        in_specs=[
            pl.BlockSpec((slots, 1), lambda i: (0, 0), pipeline_mode=pl.Buffered(1)),
            pl.BlockSpec((rows, outputs), lambda i: (0, 0), pipeline_mode=pl.Buffered(1)),
            pl.BlockSpec((outputs, tile), lambda i: (0, i)),
            pl.BlockSpec((rows, tile), lambda i: (0, i)),
        ],
        out_specs=pl.BlockSpec((owners, slots // owners, tile), lambda i: (0, 0, i)),
        out_shape=jax.ShapeDtypeStruct((owners, slots // owners, hidden), jnp.bfloat16),
        scratch_shapes=[pltpu.VMEM((slots, rows), jnp.bfloat16)],
        compiler_params=pltpu.CompilerParams(vmem_limit_bytes=VMEM_LIMIT),
        cost_estimate=pl.CostEstimate(
            flops=2 * rows * hidden * (outputs + slots),
            bytes_accessed=2 * rows * outputs + 2 * outputs * hidden + 4 * slots * hidden,
            transcendentals=rows * hidden,
        ),
        name="hidden_grad",
    )(place, grads, weight, packed)


def gather_grads(own):
    half = own.shape[0]
    pair = jnp.concatenate([own, swap(own, "b")])
    above, below = shift(pair, "x", 1), shift(pair, "x", -1)
    pair_other = swap(pair, "c")
    far_first, far_second = shift(above[:half], "x", 1), shift(below[half:], "x", -1)
    above_other, below_other = swap(above, "c"), swap(below, "c")
    far_first_other, far_second_other = swap(far_first, "c"), swap(far_second, "c")
    return jnp.concatenate(
        [
            pair,
            pair_other,
            above,
            above_other,
            below,
            below_other,
            far_first,
            far_second,
            far_first_other,
            far_second_other,
        ]
    )


def places(slots, block):
    x, b, c = (lax.axis_index(name) for name in DP)
    owner = slots // block
    away = (owner // 4 - x) % 4
    turn = jnp.where(away == 0, 0, jnp.where(away == 3, 1, away + 1))
    other_b = (owner // 2 + b) % 2
    other_c = (owner + c) % 2
    where = ((turn * 2 + other_c) * 2 + other_b) * block + slots % block
    return jnp.where(slots < 16 * block, where, 32 * block)


def reduce_to_owner(partial):
    z, a = lax.axis_index("z"), lax.axis_index("a")
    _, count, width, hidden = partial.shape

    def own(turn, side=None):
        first, many = (0, 2) if side is None else (side, 1)
        piece = lax.dynamic_slice(
            partial, (first, (z + turn) % count, 0, 0), (many, 1, width, hidden)
        )[:, 0]
        return piece if side is None else piece[0]

    def narrow(value):
        return value.astype(jnp.bfloat16)

    def wide(value):
        return value.astype(jnp.float32)

    up = shift(narrow(own(4, 0)), "z", 1)
    down = shift(narrow(own(4, 1)), "z", -1)
    up = shift(jnp.stack([narrow(own(3, 0) + wide(up)), narrow(own(3, 1))]), "z", 1)
    down = shift(jnp.stack([narrow(own(-3, 0)), narrow(own(-3, 1) + wide(down))]), "z", -1)
    up = shift(narrow(own(2) + wide(up)), "z", 1)
    down = shift(narrow(own(-2) + wide(down)), "z", -1)
    up = shift(narrow(own(1) + wide(up)), "z", 1)
    down = shift(narrow(own(-1) + wide(down)), "z", -1)
    total = own(0) + wide(up) + wide(down)
    mine = lax.dynamic_index_in_dim(total, a, 0, False)
    other = lax.dynamic_index_in_dim(total, 1 - a, 0, False)
    return mine + wide(swap(narrow(other), "a"))


def shards(patch_acts, patch_slot, out_grads, latent_weight, step_size):
    capacity, features = patch_acts.shape
    block = out_grads.shape[0]
    hidden, width = latent_weight.shape

    step_column = step_size.astype(jnp.float32).reshape(width, 1)
    latent = latent_weight.T.astype(jnp.float32)
    quantized, slope, ratio = soft_quantize(latent, step_column)
    weight = lax.all_gather(
        (step_column * quantized).astype(jnp.bfloat16), FSDP, axis=0, tiled=True
    )
    slope, pull = lax.optimization_barrier((slope, quantized - ratio * slope))

    labels = jnp.broadcast_to(patch_slot[None, :], (16, capacity))
    labels = lax.all_to_all(labels, DP, split_axis=0, concat_axis=0, tiled=True)
    place = places(labels.reshape(16 * capacity), block)

    incoming = lax.all_to_all(
        split_columns(patch_acts, 16), DP, split_axis=0, concat_axis=0, tiled=True
    ).reshape(16 * capacity, hidden)
    grads = gather_grads(out_grads)

    packed, partial = weight_grad(place.reshape(1, -1), incoming, grads)
    grad_qweight = reduce_to_owner(partial.reshape(2, 8, width, hidden))

    picked = hidden_grad(place.reshape(-1, 1), grads, weight, packed, 16)
    returned = lax.all_to_all(picked, DP, split_axis=0, concat_axis=0, tiled=True)
    grad_acts = join_columns(returned)

    grad_weight = (grad_qweight * slope).T
    share = jnp.sum(grad_qweight * pull, axis=1)
    shares = lax.all_to_all(
        jnp.broadcast_to(share[None, :], (16, width)), DP, split_axis=0, concat_axis=0, tiled=True
    )
    scale_factor = (FF_W * top_level) ** (-0.5)
    grad_step = scale_factor * jnp.sum(shares, axis=0, keepdims=True)
    return (grad_acts, grad_weight, grad_step)


def solution(mesh):
    split = Mesh(mesh.devices.reshape(SIZES), PARTS)
    return jax.shard_map(
        shards,
        mesh=split,
        in_specs=(P(PARTS, None), P(PARTS), P(PARTS, None), P(DP, FSDP), P(None, FSDP)),
        out_specs=(P(PARTS, None), P(DP, FSDP), P(None, FSDP)),
        check_vma=False,
    )
```

```python
import functools

import jax
import jax.numpy as jnp
from jax import lax
from jax.experimental import pallas as pl
from jax.experimental.pallas import tpu as pltpu
from jax.sharding import Mesh, PartitionSpec as P

FF_W = 12288

top_level = 7.0
wobble = 0.9
two_pi = 6.283185307179586
inv_root_two = 0.7071067811865476
inv_root_tau = 0.3989422804014327

PARTS = ("a", "z", "x", "b", "c")
SIZES = (2, 8, 4, 2, 2)
FSDP = ("a", "z")
DP = ("x", "b", "c")
SWAP = [(0, 1), (1, 0)]

VMEM_LIMIT = 56 * 1024 * 1024


def gelu_pair(values):
    normal_cdf = 0.5 * (1.0 + lax.erf(values * inv_root_two))
    density = jnp.exp(-0.5 * values * values) * inv_root_tau
    return (values * normal_cdf, normal_cdf + values * density)


def soft_quantize(weight, step):
    ratio = weight / step
    clipped = top_level * jnp.tanh(ratio / top_level)
    phase = two_pi * clipped
    quantized = clipped - wobble * jnp.sin(phase) / two_pi
    slope = (1.0 - wobble * jnp.cos(phase)) * (1.0 - clipped / top_level * (clipped / top_level))
    return (quantized, slope, ratio)


def swap(value, axis):
    return lax.ppermute(value, axis, SWAP)


def shift(value, axis, by):
    count = lax.axis_size(axis)
    return lax.ppermute(value, axis, [(i, (i + by) % count) for i in range(count)])


def split_columns_body(width, source, codes, target):
    rows = source.shape[0]
    for k in range(target.shape[0]):
        target[k, :rows] = source[:, k * width : (k + 1) * width]
        target[k, rows:] = codes[...]


def split_columns(values, codes, count):
    rows, width = values.shape[0], values.shape[1] // count
    many = count // 2
    tall = rows + codes.shape[0]
    return pl.pallas_call(
        functools.partial(split_columns_body, width),
        grid=(count // many,),
        in_specs=[
            pl.BlockSpec((rows, many * width), lambda i: (0, i)),
            pl.BlockSpec(codes.shape, lambda i: (0, 0)),
        ],
        out_specs=pl.BlockSpec((many, tall, width), lambda i: (i, 0, 0)),
        out_shape=jax.ShapeDtypeStruct((count, tall, width), values.dtype),
        cost_estimate=pl.CostEstimate(
            flops=0, bytes_accessed=4 * values.size, transcendentals=0
        ),
        name="split_columns",
    )(values, codes)


def join_columns_body(width, source, target):
    for k in range(source.shape[0]):
        target[:, k * width : (k + 1) * width] = source[k]


def join_columns(values):
    count, rows, width = values.shape
    many = count // 2
    return pl.pallas_call(
        functools.partial(join_columns_body, width),
        grid=(count // many,),
        in_specs=[pl.BlockSpec((many, rows, width), lambda i: (i, 0, 0))],
        out_specs=pl.BlockSpec((rows, many * width), lambda i: (0, i)),
        out_shape=jax.ShapeDtypeStruct((rows, count * width), values.dtype),
        cost_estimate=pl.CostEstimate(
            flops=0, bytes_accessed=4 * values.size, transcendentals=0
        ),
        name="join_columns",
    )(values)


def stacked(pieces):
    return jnp.concatenate([piece[...] for piece in pieces])


def contract_rows(left, right):
    return lax.dot_general(
        left, right, (((0,), (0,)), ((), ())), preferred_element_type=jnp.float32
    )


def pack_body(place, incoming, packed, act):
    part, hidden = packed.shape
    slots = place.shape[1]
    row = pl.program_id(0) * part + lax.broadcasted_iota(jnp.int32, (part, slots), 0)
    pick = jnp.where(row == place[...], 1.0, 0.0).astype(jnp.bfloat16)
    source = incoming[...].reshape(slots, hidden)
    found = jnp.dot(pick, source, preferred_element_type=jnp.float32)
    packed[...] = found.astype(jnp.bfloat16)
    act[...] = gelu_pair(found)[0].astype(jnp.bfloat16)


def pack(place, incoming, rows):
    owners, _, hidden = incoming.shape
    slots = place.shape[1]
    steps = 4
    out = pl.BlockSpec((rows // steps, hidden), lambda i: (i, 0))
    return pl.pallas_call(
        pack_body,
        grid=(steps,),
        in_specs=[
            pl.BlockSpec((1, slots), lambda i: (0, 0)),
            pl.BlockSpec(
                (owners, slots // owners, hidden),
                lambda i: (0, 0, 0),
                pipeline_mode=pl.Buffered(1),
            ),
        ],
        out_specs=[out, out],
        out_shape=[jax.ShapeDtypeStruct((rows, hidden), jnp.bfloat16)] * 2,
        compiler_params=pltpu.CompilerParams(vmem_limit_bytes=VMEM_LIMIT),
        cost_estimate=pl.CostEstimate(
            flops=2 * rows * hidden * slots,
            bytes_accessed=2 * slots * hidden + 4 * rows * hidden,
            transcendentals=rows * hidden,
        ),
        name="pack",
    )(place, incoming)


def weight_grad_body(act, *refs):
    pieces, out = refs[:-1], refs[-1]
    grad = contract_rows(stacked(pieces), act[...])
    out[...] = narrow(grad).reshape(out.shape)


def weight_grad(act, pieces, count, sides, width):
    rows, hidden = act.shape
    outputs = pieces[0].shape[1]
    steps = 4
    tile = outputs // steps
    deep = tile // width
    around = count // deep
    return pl.pallas_call(
        weight_grad_body,
        grid=(steps,),
        in_specs=[pl.BlockSpec((rows, hidden), lambda i: (0, 0), pipeline_mode=pl.Buffered(1))]
        + [pl.BlockSpec((piece.shape[0], tile), lambda i: (0, i)) for piece in pieces],
        out_specs=pl.BlockSpec(
            (deep, 1, width, hidden), lambda i: (i % around, i // around, 0, 0)
        ),
        out_shape=jax.ShapeDtypeStruct((count, sides, width, hidden), jnp.bfloat16),
        compiler_params=pltpu.CompilerParams(vmem_limit_bytes=VMEM_LIMIT),
        cost_estimate=pl.CostEstimate(
            flops=2 * rows * hidden * outputs,
            bytes_accessed=2 * rows * (outputs + hidden) + 2 * outputs * hidden,
            transcendentals=0,
        ),
        name="weight_grad",
    )(act, *pieces)


def hidden_grad_body(weight, *refs):
    pieces, total = refs[:-1], refs[-1]
    step = pl.program_id(0)
    grads = stacked(pieces)
    block = weight[...].reshape(grads.shape[1], total.shape[1])
    grad = jnp.dot(grads, block, preferred_element_type=jnp.float32)

    @pl.when(step == 0)
    def _():
        total[...] = grad

    @pl.when(step > 0)
    def _():
        total[...] += grad


def hidden_grad(pieces, weight):
    rows = sum(piece.shape[0] for piece in pieces)
    outputs = pieces[0].shape[1]
    steps = 4
    tile = outputs // steps
    count, sides, width, hidden = weight.shape
    deep = tile // width
    around = count // deep
    return pl.pallas_call(
        hidden_grad_body,
        grid=(steps,),
        in_specs=[
            pl.BlockSpec((deep, 1, width, hidden), lambda i: (i % around, i // around, 0, 0)),
        ]
        + [pl.BlockSpec((piece.shape[0], tile), lambda i: (0, i)) for piece in pieces],
        out_specs=pl.BlockSpec((rows, hidden), lambda i: (0, 0)),
        out_shape=jax.ShapeDtypeStruct((rows, hidden), jnp.float32),
        compiler_params=pltpu.CompilerParams(vmem_limit_bytes=VMEM_LIMIT),
        cost_estimate=pl.CostEstimate(
            flops=2 * rows * hidden * outputs,
            bytes_accessed=2 * rows * outputs + 2 * outputs * hidden + 4 * rows * hidden,
            transcendentals=0,
        ),
        name="hidden_grad",
    )(weight, *pieces)


def unpack_body(place, packed, grad, out, final):
    rows = packed.shape[0]
    owners, each, hidden = out.shape
    slots = owners * each

    @pl.when(pl.program_id(0) == 0)
    def _():
        slope = gelu_pair(packed[...].astype(jnp.float32))[1]
        final[...] = (grad[...] * slope).astype(jnp.bfloat16)

    column = lax.broadcasted_iota(jnp.int32, (slots, rows), 1)
    pick = jnp.where(column == place[...], 1.0, 0.0).astype(jnp.bfloat16)
    found = jnp.dot(pick, final[...], preferred_element_type=jnp.float32)
    out[...] = found.astype(jnp.bfloat16).reshape(out.shape)


def unpack(place, packed, grad, owners):
    rows, hidden = packed.shape
    slots = place.shape[0]
    steps = 4
    return pl.pallas_call(
        unpack_body,
        grid=(steps,),
        in_specs=[
            pl.BlockSpec((slots // steps, 1), lambda i: (i, 0)),
            pl.BlockSpec((rows, hidden), lambda i: (0, 0), pipeline_mode=pl.Buffered(1)),
            pl.BlockSpec((rows, hidden), lambda i: (0, 0), pipeline_mode=pl.Buffered(1)),
        ],
        out_specs=pl.BlockSpec(
            (owners // steps, slots // owners, hidden), lambda i: (i, 0, 0)
        ),
        out_shape=jax.ShapeDtypeStruct((owners, slots // owners, hidden), jnp.bfloat16),
        scratch_shapes=[pltpu.VMEM((rows, hidden), jnp.bfloat16)],
        compiler_params=pltpu.CompilerParams(vmem_limit_bytes=VMEM_LIMIT),
        cost_estimate=pl.CostEstimate(
            flops=2 * rows * hidden * slots,
            bytes_accessed=2 * slots * hidden + 6 * rows * hidden,
            transcendentals=rows * hidden,
        ),
        name="unpack",
    )(place, packed, grad)


def gather_grads(own):
    half = own.shape[0]
    pair = jnp.concatenate([own, swap(own, "b")])
    above, below = shift(pair, "x", 1), shift(pair, "x", -1)
    pair_other = swap(pair, "c")
    far_first, far_second = shift(above[:half], "x", 1), shift(below[half:], "x", -1)
    above_other, below_other = swap(above, "c"), swap(below, "c")
    far_first_other, far_second_other = swap(far_first, "c"), swap(far_second, "c")
    return [
        pair,
        pair_other,
        above,
        above_other,
        below,
        below_other,
        far_first,
        far_second,
        far_first_other,
        far_second_other,
    ]


def places(slots, block):
    x, b, c = (lax.axis_index(name) for name in DP)
    owner = slots // block
    away = (owner // 4 - x) % 4
    turn = jnp.where(away == 0, 0, jnp.where(away == 3, 1, away + 1))
    other_b = (owner // 2 + b) % 2
    other_c = (owner + c) % 2
    where = ((turn * 2 + other_c) * 2 + other_b) * block + slots % block
    return jnp.where(slots < 16 * block, where, 32 * block)


def narrow(value):
    return value.astype(jnp.bfloat16)


def wide(value):
    return value.astype(jnp.float32)


def after(value, *others):
    return lax.optimization_barrier((value, *others))[0]


def shards(patch_acts, patch_slot, out_grads, latent_weight, step_size):
    capacity, features = patch_acts.shape
    block = out_grads.shape[0]
    hidden, width = latent_weight.shape

    pieces = gather_grads(out_grads)

    step_column = wide(step_size).reshape(width, 1)
    latent = wide(latent_weight.T)
    weight = narrow(step_column * soft_quantize(latent, step_column)[0])
    weight = lax.optimization_barrier(weight)
    other = after(swap(weight, "a"), pieces[0])
    first = lax.axis_index("a") == 0
    weight = jnp.stack([jnp.where(first, weight, other), jnp.where(first, other, weight)])
    weight = lax.all_gather(weight, "z", axis=0)

    codes = jnp.concatenate([patch_slot // 32, patch_slot % 32]).astype(jnp.bfloat16)
    codes = jnp.zeros((8, hidden), jnp.bfloat16).at[0, : 2 * capacity].set(codes)
    outgoing = after(split_columns(patch_acts, codes, 16), pieces[6], pieces[7])
    incoming = lax.all_to_all(outgoing, DP, split_axis=0, concat_axis=0, tiled=True)

    latent = wide(after(latent_weight, pieces[2]).T)
    quantized, slope, ratio = soft_quantize(latent, step_column)
    slope, pull = lax.optimization_barrier((slope, quantized - ratio * slope))
    grad = hidden_grad(pieces, weight)
    incoming, grad = lax.optimization_barrier((incoming, grad))

    codes = incoming[:, capacity, : 2 * capacity].astype(jnp.int32)
    slots = codes[:, :capacity] * 32 + codes[:, capacity:]
    place = places(slots.reshape(16 * capacity), block)
    packed, act = pack(place.reshape(1, -1), incoming, 16 * block)
    partial = weight_grad(act, pieces, 8, 2, width)
    packed = after(packed, partial)
    picked = unpack(after(place, act).reshape(-1, 1), packed, grad, 16)
    summed = lax.psum_scatter(partial, "z", scatter_dimension=0, tiled=True)[0]
    a = lax.axis_index("a")
    mine = lax.dynamic_index_in_dim(summed, a, 0, False)
    other = lax.dynamic_index_in_dim(summed, 1 - a, 0, False)
    grad_qweight = wide(mine) + wide(swap(other, "a"))

    returned = lax.all_to_all(picked, DP, split_axis=0, concat_axis=0, tiled=True)
    grad_acts = join_columns(returned)

    grad_weight = (grad_qweight * slope).T
    share = after(jnp.sum(grad_qweight * pull, axis=1), returned)
    shares = lax.all_to_all(
        jnp.broadcast_to(share[None, :], (16, width)), DP, split_axis=0, concat_axis=0, tiled=True
    )
    scale_factor = (FF_W * top_level) ** (-0.5)
    grad_step = scale_factor * jnp.sum(shares, axis=0, keepdims=True)
    return (grad_acts, grad_weight, grad_step)


def solution(mesh):
    split = Mesh(mesh.devices.reshape(SIZES), PARTS)
    return jax.shard_map(
        shards,
        mesh=split,
        in_specs=(P(PARTS, None), P(PARTS), P(PARTS, None), P(DP, FSDP), P(None, FSDP)),
        out_specs=(P(PARTS, None), P(DP, FSDP), P(None, FSDP)),
        check_vma=False,
    )
```

```python
import functools

import jax
import jax.numpy as jnp
from jax import lax
from jax.experimental import pallas as pl
from jax.experimental.pallas import tpu as pltpu
from jax.sharding import Mesh, PartitionSpec as P

FF_W = 12288

top_level = 7.0
wobble = 0.9
two_pi = 6.283185307179586
inv_root_two = 0.7071067811865476
inv_root_tau = 0.3989422804014327

PARTS = ("a", "z", "x", "b", "c")
SIZES = (2, 8, 4, 2, 2)
FSDP = ("a", "z")
DP = ("x", "b", "c")
SWAP = [(0, 1), (1, 0)]

ON_CHIP = pl.BlockSpec(memory_space=pltpu.VMEM)
LARGE_VMEM = pltpu.CompilerParams(vmem_limit_bytes=50 * 1024 * 1024)
SMALL_VMEM = pltpu.CompilerParams(vmem_limit_bytes=24 * 1024 * 1024)


def gelu_pair(values):
    normal_cdf = 0.5 * (1.0 + lax.erf(values * inv_root_two))
    density = jnp.exp(-0.5 * values * values) * inv_root_tau
    return (values * normal_cdf, normal_cdf + values * density)


def soft_quantize(weight, step):
    ratio = weight / step
    clipped = top_level * jnp.tanh(ratio / top_level)
    phase = two_pi * clipped
    quantized = clipped - wobble * jnp.sin(phase) / two_pi
    slope = (1.0 - wobble * jnp.cos(phase)) * (1.0 - clipped / top_level * (clipped / top_level))
    return (quantized, slope, ratio)


def swap(value, axis):
    return lax.ppermute(value, axis, SWAP)


def shift(value, axis, by):
    count = lax.axis_size(axis)
    return lax.ppermute(value, axis, [(i, (i + by) % count) for i in range(count)])


def split_columns_body(width, source, codes, target):
    rows = source.shape[0]
    for k in range(target.shape[0]):
        target[k, :rows] = source[:, k * width : (k + 1) * width]
        target[k, rows:] = codes[...]


def split_columns(values, codes, count):
    rows, width = values.shape[0], values.shape[1] // count
    many = count // 2
    tall = rows + codes.shape[0]
    return pl.pallas_call(
        functools.partial(split_columns_body, width),
        grid=(count // many,),
        in_specs=[
            pl.BlockSpec((rows, many * width), lambda i: (0, i)),
            pl.BlockSpec(codes.shape, lambda i: (0, 0)),
        ],
        out_specs=pl.BlockSpec((many, tall, width), lambda i: (i, 0, 0)),
        out_shape=jax.ShapeDtypeStruct((count, tall, width), values.dtype),
        cost_estimate=pl.CostEstimate(
            flops=0, bytes_accessed=4 * values.size, transcendentals=0
        ),
        name="split_columns",
    )(values, codes)


def join_columns_body(width, source, target):
    many = target.shape[1] // width
    first = pl.program_id(0) * many
    for k in range(many):
        target[:, k * width : (k + 1) * width] = source[first + k]


def join_columns(values):
    count, rows, width = values.shape
    many = count // 2
    return pl.pallas_call(
        functools.partial(join_columns_body, width),
        grid=(count // many,),
        in_specs=[ON_CHIP],
        out_specs=pl.BlockSpec((rows, many * width), lambda i: (0, i)),
        out_shape=jax.ShapeDtypeStruct((rows, count * width), values.dtype),
        compiler_params=SMALL_VMEM,
        cost_estimate=pl.CostEstimate(
            flops=0, bytes_accessed=4 * values.size, transcendentals=0
        ),
        name="join_columns",
    )(values)


def contract_rows(left, right):
    return lax.dot_general(
        left, right, (((0,), (0,)), ((), ())), preferred_element_type=jnp.float32
    )


def pack_body(place, incoming, packed, act):
    part, hidden = 256, packed.shape[1]
    slots = place.shape[1]
    each = slots // incoming.shape[0]
    start = pl.multiple_of(pl.program_id(0) * part, part)
    row = start + lax.broadcasted_iota(jnp.int32, (part, slots), 0)
    pick = jnp.where(row == place[...], 1.0, 0.0).astype(jnp.bfloat16)
    source = incoming[:, :each, :].reshape(slots, hidden)
    found = jnp.dot(pick, source, preferred_element_type=jnp.float32)
    packed[pl.ds(start, part), :] = narrow(found)
    act[pl.ds(start, part), :] = narrow(gelu_pair(found)[0])


def pack(place, incoming, rows):
    hidden = incoming.shape[2]
    slots = place.shape[1]
    return pl.pallas_call(
        pack_body,
        grid=(rows // 256,),
        in_specs=[pl.BlockSpec((1, slots), lambda i: (0, 0)), ON_CHIP],
        out_specs=[ON_CHIP, ON_CHIP],
        out_shape=[jax.ShapeDtypeStruct((rows, hidden), jnp.bfloat16)] * 2,
        compiler_params=SMALL_VMEM,
        cost_estimate=pl.CostEstimate(
            flops=2 * rows * hidden * slots,
            bytes_accessed=2 * slots * hidden + 4 * rows * hidden,
            transcendentals=rows * hidden,
        ),
        name="pack",
    )(place, incoming)


def stacked(pieces):
    return jnp.concatenate([piece[...] for piece in pieces])


def weight_grad_body(act, *refs):
    pieces, out = refs[:-1], refs[-1]
    grad = contract_rows(stacked(pieces), act[...])
    out[...] = narrow(grad).reshape(out.shape)


def weight_grad(act, pieces, count, sides, width):
    rows, hidden = act.shape
    outputs = pieces[0].shape[1]
    steps = 4
    deep = outputs // steps // width
    around = count // deep
    return pl.pallas_call(
        weight_grad_body,
        grid=(steps,),
        in_specs=[ON_CHIP]
        + [pl.BlockSpec((piece.shape[0], outputs // steps), lambda i: (0, i)) for piece in pieces],
        out_specs=pl.BlockSpec(
            (deep, 1, width, hidden), lambda i: (i % around, i // around, 0, 0)
        ),
        out_shape=jax.ShapeDtypeStruct((count, sides, width, hidden), jnp.bfloat16),
        compiler_params=LARGE_VMEM,
        cost_estimate=pl.CostEstimate(
            flops=2 * rows * hidden * outputs,
            bytes_accessed=2 * rows * (outputs + hidden) + 2 * outputs * hidden,
            transcendentals=0,
        ),
        name="weight_grad",
    )(act, *pieces)


def near_grad_body(weight, *refs):
    pieces, total = refs[:-1], refs[-1]
    step = pl.program_id(0)
    tile = weight.shape[0] * weight.shape[2]
    grads = stacked(pieces)
    block = weight[...].reshape(tile, total.shape[1])
    grad = jnp.dot(grads, block, preferred_element_type=jnp.float32)

    @pl.when(step == 0)
    def _():
        total[...] = grad

    @pl.when(step > 0)
    def _():
        total[...] += grad


def hidden_specs(pieces, weight, steps):
    tile = pieces[0].shape[1] // steps
    count, sides, width, hidden = weight.shape
    deep = tile // width
    around = count // deep
    return [
        pl.BlockSpec((deep, 1, width, hidden), lambda i: (i % around, i // around, 0, 0)),
    ] + [pl.BlockSpec((piece.shape[0], tile), lambda i: (0, i)) for piece in pieces]


def hidden_cost(rows, weight, transcendentals):
    hidden = weight.shape[-1]
    outputs = weight.size // hidden
    return pl.CostEstimate(
        flops=2 * rows * hidden * outputs,
        bytes_accessed=2 * rows * outputs + 2 * outputs * hidden + 4 * rows * hidden,
        transcendentals=transcendentals,
    )


def near_grad(pieces, weight):
    rows = sum(piece.shape[0] for piece in pieces)
    hidden = weight.shape[-1]
    steps = 4
    return pl.pallas_call(
        near_grad_body,
        grid=(steps,),
        in_specs=hidden_specs(pieces, weight, steps),
        out_specs=ON_CHIP,
        out_shape=jax.ShapeDtypeStruct((rows, hidden), jnp.float32),
        compiler_params=LARGE_VMEM,
        cost_estimate=hidden_cost(rows, weight, 0),
        name="near_grad",
    )(weight, *pieces)


def hidden_grad_body(steps, packed, near, weight, *refs):
    pieces, (out, total) = refs[:-2], refs[-2:]
    step = pl.program_id(0)
    rows = near.shape[0]

    def slope(some):
        return gelu_pair(wide(packed[some, :]))[1]

    part = rows // steps
    some = pl.ds(pl.multiple_of(step * part, part), part)
    out[some, :] = narrow(near[some, :] * slope(some))

    tile = weight.shape[0] * weight.shape[2]
    grads = stacked(pieces)
    block = weight[...].reshape(tile, total.shape[1])
    grad = jnp.dot(grads, block, preferred_element_type=jnp.float32)

    @pl.when(step == 0)
    def _():
        total[...] = grad

    @pl.when((step > 0) & (step < steps - 1))
    def _():
        total[...] += grad

    @pl.when(step == steps - 1)
    def _():
        rest = pl.ds(rows, total.shape[0])
        out[rest, :] = narrow((total[...] + grad) * slope(rest))


def hidden_grad(packed, near, pieces, weight):
    rows = sum(piece.shape[0] for piece in pieces)
    total, hidden = near.shape[0] + rows, weight.shape[-1]
    steps = 4
    return pl.pallas_call(
        functools.partial(hidden_grad_body, steps),
        grid=(steps,),
        in_specs=[ON_CHIP, ON_CHIP] + hidden_specs(pieces, weight, steps),
        out_specs=ON_CHIP,
        out_shape=jax.ShapeDtypeStruct((total, hidden), jnp.bfloat16),
        scratch_shapes=[pltpu.VMEM((rows, hidden), jnp.float32)],
        compiler_params=LARGE_VMEM,
        cost_estimate=hidden_cost(rows, weight, total * hidden),
        name="hidden_grad",
    )(packed, near, weight, *pieces)


def unpack_body(place, grad, out):
    slots, rows = place.shape[0], grad.shape[0]
    column = lax.broadcasted_iota(jnp.int32, (slots, rows), 1)
    pick = jnp.where(column == place[...], 1.0, 0.0).astype(jnp.bfloat16)
    found = jnp.dot(pick, grad[...], preferred_element_type=jnp.float32)
    out[...] = narrow(found).reshape(out.shape)


def unpack(place, grad, owners):
    rows, hidden = grad.shape
    slots = place.shape[0]
    steps = 4
    return pl.pallas_call(
        unpack_body,
        grid=(steps,),
        in_specs=[
            pl.BlockSpec((slots // steps, 1), lambda i: (i, 0)),
            ON_CHIP,
        ],
        out_specs=pl.BlockSpec(
            (owners // steps, slots // owners, hidden), lambda i: (i, 0, 0)
        ),
        out_shape=jax.ShapeDtypeStruct((owners, slots // owners, hidden), jnp.bfloat16),
        compiler_params=SMALL_VMEM,
        cost_estimate=pl.CostEstimate(
            flops=2 * rows * hidden * slots,
            bytes_accessed=2 * slots * hidden + 2 * rows * hidden,
            transcendentals=0,
        ),
        name="unpack",
    )(place, grad)


def gather_near(own, first):
    half = own.shape[0]
    pair = after(jnp.concatenate([own, swap(own, "b")]), first)
    above, below = shift(pair, "x", 1), shift(pair, "x", -1)
    near = [pair, swap(pair, "c"), above, swap(above, "c"), below, swap(below, "c")]
    ends = lax.optimization_barrier((above[:half], below[half:]))
    return near, ends


def gather_far(ends, first):
    far_first, far_second = shift(ends[0], "x", 1), shift(ends[1], "x", -1)
    far_first, far_second, _ = lax.optimization_barrier((far_first, far_second, first))
    return [far_first, far_second, swap(far_first, "c"), swap(far_second, "c")]


def places(slots, block):
    x, b, c = (lax.axis_index(name) for name in DP)
    owner = slots // block
    away = (owner // 4 - x) % 4
    turn = jnp.where(away == 0, 0, jnp.where(away == 3, 1, away + 1))
    other_b = (owner // 2 + b) % 2
    other_c = (owner + c) % 2
    where = ((turn * 2 + other_c) * 2 + other_b) * block + slots % block
    return jnp.where(slots < 16 * block, where, 32 * block)


def narrow(value):
    return value.astype(jnp.bfloat16)


def wide(value):
    return value.astype(jnp.float32)


def after(value, *others):
    return lax.optimization_barrier((value, *others))[0]


def shards(patch_acts, patch_slot, out_grads, latent_weight, step_size):
    capacity, features = patch_acts.shape
    block = out_grads.shape[0]
    hidden, width = latent_weight.shape

    a = lax.axis_index("a")

    codes = jnp.concatenate([patch_slot // 32, patch_slot % 32]).astype(jnp.bfloat16)
    codes = jnp.zeros((8, hidden), jnp.bfloat16).at[0, : 2 * capacity].set(codes)
    outgoing = split_columns(patch_acts, codes, 16)
    near, ends = gather_near(out_grads, outgoing)

    step_column = wide(step_size).reshape(width, 1)
    latent = wide(latent_weight.T)
    weight = narrow(step_column * soft_quantize(latent, step_column)[0])
    weight = lax.optimization_barrier(weight)
    other = after(swap(weight, "a"), near[0])
    weight = jnp.stack([jnp.where(a == 0, weight, other), jnp.where(a == 0, other, weight)])
    weight = lax.all_gather(weight, "z", axis=0)

    latent = wide(after(latent_weight, near[0]).T)
    quantized, slope, ratio = soft_quantize(latent, step_column)
    slope, pull = lax.optimization_barrier((slope, quantized - ratio * slope))
    pull_other = swap(pull, "a")

    outgoing = after(outgoing, *ends, pull_other)
    incoming = lax.all_to_all(outgoing, DP, split_axis=0, concat_axis=0, tiled=True)
    near_part = near_grad(near, weight)
    incoming, near_part = lax.optimization_barrier((incoming, near_part))

    codes = incoming[:, capacity, : 2 * capacity].astype(jnp.int32)
    slots = codes[:, :capacity] * 32 + codes[:, capacity:]
    place = places(slots.reshape(16 * capacity), block)
    packed, act = pack(place.reshape(1, -1), incoming, 16 * block)
    far = gather_far(ends, act)
    column = after(place, act).reshape(-1, 1)
    partial = weight_grad(after(act, column), near + far, 8, 2, width)
    summed = lax.psum_scatter(partial, "z", scatter_dimension=0, tiled=True)[0]

    grad = hidden_grad(after(packed, partial), near_part, far, weight)
    picked = unpack(column, grad, 16)
    returned = lax.all_to_all(picked, DP, split_axis=0, concat_axis=0, tiled=True)
    grad_acts = join_columns(returned)

    mine = lax.dynamic_index_in_dim(summed, a, 0, False)
    other = lax.dynamic_index_in_dim(summed, 1 - a, 0, False)
    share = jnp.sum(wide(mine) * pull, axis=1)
    share_other = jnp.sum(wide(other) * pull_other, axis=1)
    shares = jnp.stack([jnp.where(a == 0, share, share_other), jnp.where(a == 0, share_other, share)])
    shares = jnp.broadcast_to(after(shares, returned)[:, None], (2, 16, width)).reshape(32, width)
    shares = lax.all_to_all(shares, ("a",) + DP, split_axis=0, concat_axis=0, tiled=True)

    grad_qweight = wide(mine) + wide(swap(other, "a"))
    grad_weight = (grad_qweight * slope).T
    shares = after(shares, grad_weight)
    scale_factor = (FF_W * top_level) ** (-0.5)
    grad_step = scale_factor * jnp.sum(shares, axis=0, keepdims=True)
    return (grad_acts, grad_weight, grad_step)


def solution(mesh):
    split = Mesh(mesh.devices.reshape(SIZES), PARTS)
    return jax.shard_map(
        shards,
        mesh=split,
        in_specs=(P(PARTS, None), P(PARTS), P(PARTS, None), P(DP, FSDP), P(None, FSDP)),
        out_specs=(P(PARTS, None), P(DP, FSDP), P(None, FSDP)),
        check_vma=False,
    )
```

```python
import functools

import jax
import jax.numpy as jnp
from jax import lax
from jax.experimental import pallas as pl
from jax.experimental.pallas import tpu as pltpu
from jax.sharding import Mesh, PartitionSpec as P

FF_W = 12288

top_level = 7.0
wobble = 0.9
two_pi = 6.283185307179586
inv_root_two = 0.7071067811865476
inv_root_tau = 0.3989422804014327

PARTS = ("a", "z", "x", "b", "c")
SIZES = (2, 8, 4, 2, 2)
FSDP = ("a", "z")
DP = ("x", "b", "c")
SWAP = [(0, 1), (1, 0)]

ON_CHIP = pl.BlockSpec(memory_space=pltpu.VMEM)


def vmem(mebibytes):
    return pltpu.CompilerParams(vmem_limit_bytes=mebibytes * 1024 * 1024)


LARGE_VMEM = pltpu.CompilerParams(vmem_limit_bytes=50 * 1024 * 1024)
SMALL_VMEM = pltpu.CompilerParams(vmem_limit_bytes=24 * 1024 * 1024)


def gelu_pair(values):
    normal_cdf = 0.5 * (1.0 + lax.erf(values * inv_root_two))
    density = jnp.exp(-0.5 * values * values) * inv_root_tau
    return (values * normal_cdf, normal_cdf + values * density)


def soft_quantize(weight, step):
    ratio = weight / step
    clipped = top_level * jnp.tanh(ratio / top_level)
    phase = two_pi * clipped
    quantized = clipped - wobble * jnp.sin(phase) / two_pi
    slope = (1.0 - wobble * jnp.cos(phase)) * (1.0 - clipped / top_level * (clipped / top_level))
    return (quantized, slope, ratio)


def swap(value, axis):
    return lax.ppermute(value, axis, SWAP)


def shift(value, axis, by):
    count = lax.axis_size(axis)
    return lax.ppermute(value, axis, [(i, (i + by) % count) for i in range(count)])


def split_columns_body(width, source, codes, target):
    rows = source.shape[0]
    for k in range(target.shape[0]):
        target[k, :rows] = source[:, k * width : (k + 1) * width]
        target[k, rows:] = codes[...]


def split_columns(values, codes, count):
    rows, width = values.shape[0], values.shape[1] // count
    many = count // 2
    tall = rows + codes.shape[0]
    return pl.pallas_call(
        functools.partial(split_columns_body, width),
        grid=(count // many,),
        in_specs=[
            pl.BlockSpec((rows, many * width), lambda i: (0, i)),
            pl.BlockSpec(codes.shape, lambda i: (0, 0)),
        ],
        out_specs=pl.BlockSpec((many, tall, width), lambda i: (i, 0, 0)),
        out_shape=jax.ShapeDtypeStruct((count, tall, width), values.dtype),
        cost_estimate=pl.CostEstimate(
            flops=0, bytes_accessed=4 * values.size, transcendentals=0
        ),
        name="split_columns",
    )(values, codes)


def join_columns_body(width, source, target):
    many = target.shape[1] // width
    first = pl.program_id(0) * many
    for k in range(many):
        target[:, k * width : (k + 1) * width] = source[first + k]


def join_columns(values):
    count, rows, width = values.shape
    many = count // 2
    return pl.pallas_call(
        functools.partial(join_columns_body, width),
        grid=(count // many,),
        in_specs=[ON_CHIP],
        out_specs=pl.BlockSpec((rows, many * width), lambda i: (0, i)),
        out_shape=jax.ShapeDtypeStruct((rows, count * width), values.dtype),
        compiler_params=vmem(24),
        cost_estimate=pl.CostEstimate(
            flops=0, bytes_accessed=4 * values.size, transcendentals=0
        ),
        name="join_columns",
    )(values)


def contract_rows(left, right):
    return lax.dot_general(
        left, right, (((0,), (0,)), ((), ())), preferred_element_type=jnp.float32
    )


def pack_body(place, incoming, packed, act, token):
    part, hidden = 256, packed.shape[1]
    slots = place.shape[1]
    each = slots // incoming.shape[0]
    start = pl.multiple_of(pl.program_id(0) * part, part)
    row = start + lax.broadcasted_iota(jnp.int32, (part, slots), 0)
    pick = jnp.where(row == place[...], 1.0, 0.0).astype(jnp.bfloat16)
    source = incoming[:, :each, :].reshape(slots, hidden)
    found = jnp.dot(pick, source, preferred_element_type=jnp.float32)
    packed[pl.ds(start, part), :] = narrow(found)
    act[pl.ds(start, part), :] = narrow(gelu_pair(found)[0])
    token[...] = found[:8, :128]


def pack(place, incoming, rows):
    hidden = incoming.shape[2]
    slots = place.shape[1]
    return pl.pallas_call(
        pack_body,
        grid=(rows // 256,),
        in_specs=[pl.BlockSpec((1, slots), lambda i: (0, 0)), ON_CHIP],
        out_specs=[ON_CHIP, ON_CHIP, pl.BlockSpec((8, 128), lambda i: (0, 0))],
        out_shape=[jax.ShapeDtypeStruct((rows, hidden), jnp.bfloat16)] * 2
        + [jax.ShapeDtypeStruct((8, 128), jnp.float32)],
        compiler_params=vmem(40),
        cost_estimate=pl.CostEstimate(
            flops=2 * rows * hidden * slots,
            bytes_accessed=2 * slots * hidden + 4 * rows * hidden,
            transcendentals=rows * hidden,
        ),
        name="pack",
    )(place, incoming)


def stacked(pieces):
    return jnp.concatenate([piece[...] for piece in pieces])


def weight_grad_body(act, *refs):
    pieces, out = refs[:-1], refs[-1]
    grad = contract_rows(stacked(pieces), act[...])
    out[...] = narrow(grad).reshape(out.shape)


def weight_grad(act, pieces, count, sides, width):
    rows, hidden = act.shape
    outputs = pieces[0].shape[1]
    steps = 4
    deep = outputs // steps // width
    around = count // deep
    return pl.pallas_call(
        weight_grad_body,
        grid=(steps,),
        in_specs=[ON_CHIP]
        + [pl.BlockSpec((piece.shape[0], outputs // steps), lambda i: (0, i)) for piece in pieces],
        out_specs=pl.BlockSpec(
            (deep, 1, width, hidden), lambda i: (i % around, i // around, 0, 0)
        ),
        out_shape=jax.ShapeDtypeStruct((count, sides, width, hidden), jnp.bfloat16),
        compiler_params=vmem(52),
        cost_estimate=pl.CostEstimate(
            flops=2 * rows * hidden * outputs,
            bytes_accessed=2 * rows * (outputs + hidden) + 2 * outputs * hidden,
            transcendentals=0,
        ),
        name="weight_grad",
    )(act, *pieces)


def hidden_grad_body(steps, packed, weight, *refs):
    pieces, (out, slope, total) = refs[:-3], refs[-3:]
    step = pl.program_id(0)

    part = slope.shape[0] // steps
    some = pl.ds(pl.multiple_of(step * part, part), part)
    slope[some, :] = gelu_pair(wide(packed[some, :]))[1]

    grads = stacked(pieces)
    block = weight[...].reshape(grads.shape[1], total.shape[1])
    grad = jnp.dot(grads, block, preferred_element_type=jnp.float32)

    @pl.when(step == 0)
    def _():
        total[...] = grad

    @pl.when((step > 0) & (step < steps - 1))
    def _():
        total[...] += grad

    @pl.when(step == steps - 1)
    def _():
        out[...] = narrow((total[...] + grad) * slope[...])


def hidden_grad(packed, pieces, weight):
    rows = sum(piece.shape[0] for piece in pieces)
    outputs = pieces[0].shape[1]
    steps = 4
    tile = outputs // steps
    count, sides, width, hidden = weight.shape
    deep = tile // width
    around = count // deep
    return pl.pallas_call(
        functools.partial(hidden_grad_body, steps),
        grid=(steps,),
        in_specs=[
            pl.BlockSpec((rows, hidden), lambda i: (0, 0), pipeline_mode=pl.Buffered(1)),
            pl.BlockSpec((deep, 1, width, hidden), lambda i: (i % around, i // around, 0, 0)),
        ]
        + [pl.BlockSpec((piece.shape[0], tile), lambda i: (0, i)) for piece in pieces],
        out_specs=pl.BlockSpec((rows, hidden), lambda i: (0, 0)),
        out_shape=jax.ShapeDtypeStruct((rows, hidden), jnp.bfloat16),
        scratch_shapes=[
            pltpu.VMEM((rows, hidden), jnp.float32),
            pltpu.VMEM((rows, hidden), jnp.float32),
        ],
        compiler_params=vmem(54),
        cost_estimate=pl.CostEstimate(
            flops=2 * rows * hidden * outputs,
            bytes_accessed=2 * rows * outputs + 2 * outputs * hidden + 4 * rows * hidden,
            transcendentals=rows * hidden,
        ),
        name="hidden_grad",
    )(packed, weight, *pieces)


def unpack_body(place, grad, out):
    slots, rows = place.shape[0], grad.shape[0]
    column = lax.broadcasted_iota(jnp.int32, (slots, rows), 1)
    pick = jnp.where(column == place[...], 1.0, 0.0).astype(jnp.bfloat16)
    found = jnp.dot(pick, grad[...], preferred_element_type=jnp.float32)
    out[...] = narrow(found).reshape(out.shape)


def unpack(place, grad, owners):
    rows, hidden = grad.shape
    slots = place.shape[0]
    steps = 4
    return pl.pallas_call(
        unpack_body,
        grid=(steps,),
        in_specs=[
            pl.BlockSpec((slots // steps, 1), lambda i: (i, 0)),
            ON_CHIP,
        ],
        out_specs=pl.BlockSpec(
            (owners // steps, slots // owners, hidden), lambda i: (i, 0, 0)
        ),
        out_shape=jax.ShapeDtypeStruct((owners, slots // owners, hidden), jnp.bfloat16),
        compiler_params=vmem(54),
        cost_estimate=pl.CostEstimate(
            flops=2 * rows * hidden * slots,
            bytes_accessed=2 * slots * hidden + 2 * rows * hidden,
            transcendentals=0,
        ),
        name="unpack",
    )(place, grad)


def gather_near(own, first):
    half = own.shape[0]
    pair = after(jnp.concatenate([own, swap(own, "b")]), first)
    above, below = shift(pair, "x", 1), shift(pair, "x", -1)
    near = [pair, swap(pair, "c"), above, swap(above, "c"), below, swap(below, "c")]
    ends = lax.optimization_barrier((above[:half], below[half:]))
    return near, ends


def gather_far(ends, first):
    far_first, far_second = shift(ends[0], "x", 1), shift(ends[1], "x", -1)
    far_first, far_second, _ = lax.optimization_barrier((far_first, far_second, first))
    return [far_first, far_second, swap(far_first, "c"), swap(far_second, "c")]


def places(slots, block):
    x, b, c = (lax.axis_index(name) for name in DP)
    owner = slots // block
    away = (owner // 4 - x) % 4
    turn = jnp.where(away == 0, 0, jnp.where(away == 3, 1, away + 1))
    other_b = (owner // 2 + b) % 2
    other_c = (owner + c) % 2
    where = ((turn * 2 + other_c) * 2 + other_b) * block + slots % block
    return jnp.where(slots < 16 * block, where, 32 * block)


def narrow(value):
    return value.astype(jnp.bfloat16)


def wide(value):
    return value.astype(jnp.float32)


def after(value, *others):
    return lax.optimization_barrier((value, *others))[0]


def shards(patch_acts, patch_slot, out_grads, latent_weight, step_size):
    capacity, features = patch_acts.shape
    block = out_grads.shape[0]
    hidden, width = latent_weight.shape

    a = lax.axis_index("a")

    codes = jnp.concatenate([patch_slot // 32, patch_slot % 32]).astype(jnp.bfloat16)
    codes = jnp.zeros((8, hidden), jnp.bfloat16).at[0, : 2 * capacity].set(codes)
    outgoing = split_columns(patch_acts, codes, 16)
    near, ends = gather_near(out_grads, outgoing)

    step_column = wide(step_size).reshape(width, 1)
    latent = wide(latent_weight.T)
    weight = narrow(step_column * soft_quantize(latent, step_column)[0])
    weight = lax.optimization_barrier(weight)
    other = after(swap(weight, "a"), near[2], near[4])
    weight = jnp.stack([jnp.where(a == 0, weight, other), jnp.where(a == 0, other, weight)])
    weight = lax.all_gather(weight, "z", axis=0)

    latent = wide(after(latent_weight, near[2], near[4]).T)
    quantized, slope, ratio = soft_quantize(latent, step_column)
    slope, pull = lax.optimization_barrier((slope, quantized - ratio * slope))
    pull_other = swap(pull, "a")

    outgoing = after(outgoing, *ends)
    incoming = lax.all_to_all(outgoing, DP, split_axis=0, concat_axis=0, tiled=True)
    codes = incoming[:, capacity, : 2 * capacity].astype(jnp.int32)
    slots = codes[:, :capacity] * 32 + codes[:, capacity:]
    place = places(slots.reshape(16 * capacity), block)
    packed, act, token = pack(place.reshape(1, -1), incoming, 16 * block)
    far = gather_far(ends, token)
    column = after(place, token).reshape(-1, 1)
    partial = weight_grad(after(act, column), near + far, 8, 2, width)
    summed = lax.psum_scatter(partial, "z", scatter_dimension=0, tiled=True)[0]

    grad = hidden_grad(packed, near + far, after(weight, partial, pull_other))
    picked = unpack(column, grad, 16)
    returned = lax.all_to_all(picked, DP, split_axis=0, concat_axis=0, tiled=True)
    grad_acts = join_columns(returned)

    mine = lax.dynamic_index_in_dim(summed, a, 0, False)
    other = lax.dynamic_index_in_dim(summed, 1 - a, 0, False)
    share = jnp.sum(wide(mine) * pull, axis=1)
    share_other = jnp.sum(wide(other) * pull_other, axis=1)
    shares = jnp.stack([jnp.where(a == 0, share, share_other), jnp.where(a == 0, share_other, share)])
    shares = jnp.broadcast_to(after(shares, returned)[:, None], (2, 16, width)).reshape(32, width)
    shares = lax.all_to_all(shares, ("a",) + DP, split_axis=0, concat_axis=0, tiled=True)

    grad_qweight = wide(mine) + wide(swap(other, "a"))
    grad_weight = (grad_qweight * slope).T
    shares = after(shares, grad_weight)
    scale_factor = (FF_W * top_level) ** (-0.5)
    grad_step = scale_factor * jnp.sum(shares, axis=0, keepdims=True)
    return (grad_acts, grad_weight, grad_step)


def solution(mesh):
    split = Mesh(mesh.devices.reshape(SIZES), PARTS)
    return jax.shard_map(
        shards,
        mesh=split,
        in_specs=(P(PARTS, None), P(PARTS), P(PARTS, None), P(DP, FSDP), P(None, FSDP)),
        out_specs=(P(PARTS, None), P(DP, FSDP), P(None, FSDP)),
        check_vma=False,
    )
```
